32 devices in a mesh: grp: 2 (over y), pb: 16 (over z, x, core).
Axes of the slice: x: 2, y: 2, z: 4, core: 2. Of those that a mesh axis runs over, the one named last changes fastest.
Arguments:
- queries: bfloat16 [4096, 2048], P('pb', 'grp'), parts along dimension 1, may hold values from -150 to 150
- keys: bfloat16 [4096, 256], P('pb', 'grp'), parts along dimension 1, may hold values from -6 to 6
- values: bfloat16 [4096, 256], P('pb', 'grp'), parts along dimension 1, may hold values from -6 to 6
- basis: bfloat16 [256, 128], P('grp'), parts along dimension 0, may hold values from -0.5 to 0.5
- picks: int32 [64, 16], P('grp'), parts along dimension 0, may hold values from -1 to 7, as said below
Outputs:
- attended: bfloat16 [4096, 2048], P('pb', 'grp'), parts along dimension 1
The draws below stay inside these ranges and needn't reach their ends.
There are 2 independent parts, one for each index of `grp`. The reference program is written for one: setup_inputs(seed, part) draws one part's arguments, and reference() takes and returns one part's arrays. A program takes and returns all parts, laid end to end along the dimension named above; each array names one. Nothing has to cross between parts.
Inputs may be any that keep to these rules, and one draw needn't show every extreme that they name: picks[b, s] is -1 when neither block of device s (blocks s and 31 - s) ends before block b - 1 begins; else it names a sub-block of one of those blocks that lies wholly before block b - 1.
All inputs are finite; a program needn't handle non-finite values.
Results may differ from the reference program's by a relative error of at most 0.011.
Values may be sent and summed in bfloat16 or wider, within the bound.
A program may use at most 64 MiB of HBM per device.

```python
import jax
import jax.numpy as jnp
from jax import lax

HQ = 8
HD = 128
KB = 32
H = 128
NBLK = 32
SEQ = 4096


def draw_picks(key, part):
    sources = NBLK // 2
    per_block = H // KB
    block = jnp.arange(NBLK, dtype=jnp.int32)[:, None]
    source = jnp.arange(sources, dtype=jnp.int32)[None, :]
    early_ok = source < block - 1
    late_ok = NBLK - 1 - source < block - 1
    first, second = jax.random.split(jax.random.fold_in(key, 7))
    coin = jax.random.randint(first, (NBLK, sources), 0, 2)
    within = jax.random.randint(second, (NBLK, sources), 0, per_block)
    use_late = late_ok & (jnp.logical_not(early_ok) | (coin == 1))
    use_early = early_ok & jnp.logical_not(use_late)
    return jnp.where(use_late, per_block + within, jnp.where(use_early, within, -1)).astype(jnp.int32)


def draw_queries(key, part):
    shape = (NBLK * H, HQ * HD)
    first = jax.random.fold_in(jax.random.fold_in(key, 11), 0)
    return jnp.clip(jax.random.normal(first, shape, jnp.float32) * 2.0, -12.0, 12.0).astype(jnp.bfloat16)


def shard_levels(stream_key, shape, shards, least, high):
    gain, own = 1.0, jax.random.fold_in(stream_key, 6)
    for position, parts in shards:
        draws = jnp.exp(jax.random.uniform(jax.random.fold_in(own, position), (parts,), jnp.float32, least / len(shards), high / len(shards)))
        gain = gain * jnp.repeat(draws, shape[position] // parts).reshape([-1 if axis == position else 1 for axis in range(len(shape))])
    return gain


def gaussian(key, shape, scale, limit, cuts=(), kind=jnp.bfloat16):
    factor_of = shard_levels(key, shape, cuts, -0.22, 0.18) if cuts else 1.0
    drawn = jax.random.normal(key, shape, jnp.float32) * scale * factor_of
    return jnp.minimum(jnp.maximum(drawn, -limit), limit).astype(kind)


def setup_inputs(seed: int = 0, part: int = 0) -> dict:
    streams_of = jax.random.split(jax.random.key(seed), 6)
    own_keys = jax.random.split(jax.random.fold_in(streams_of[5], part), 6)
    return {
        "queries": draw_queries(jax.random.fold_in(jax.random.fold_in(streams_of[5], part), 71), part),
        "keys": gaussian(own_keys[1], (SEQ, HD), 1.0, 6.0, ((0, 16),)),
        "values": gaussian(own_keys[2], (SEQ, HD), 1.0, 6.0, ((0, 16),)),
        "basis": gaussian(own_keys[3], (HD, HD), HD ** -0.5, 0.5),
        "picks": draw_picks(jax.random.fold_in(jax.random.fold_in(streams_of[5], part), 71), part),
    }


def block_start(block, half):
    count = NBLK // 2
    early = block < count
    device = jnp.where(early, block, NBLK - 1 - block)
    return (device * 2 * half + jnp.where(early, 0, half)).astype(jnp.int32)


def attend(q_rot, chosen, chosen_ok, own):
    nq = q_rot.shape[0]
    dim = q_rot.shape[2]
    keys_all = jnp.concatenate([chosen[:, :dim], own[:, :dim]], axis=0)
    vals_all = jnp.concatenate([chosen[:, dim:], own[:, dim:]], axis=0)
    causal = jnp.arange(nq)[:, None] >= jnp.arange(nq)[None, :]
    usable = jnp.concatenate([jnp.broadcast_to(chosen_ok[None, :], (nq, chosen.shape[0])), causal], axis=1)
    scores = jnp.einsum('qhd,kd->hqk', q_rot.astype(jnp.float32), keys_all.astype(jnp.float32)) * (dim ** -0.5)
    scores = jnp.where(usable[None], scores, jnp.float32(-1e30))
    top = jnp.max(scores, axis=-1, keepdims=True)
    weight = jnp.exp(scores - top)
    total = jnp.sum(weight, axis=-1)
    weight_b = weight.astype(jnp.bfloat16)
    summed = jnp.einsum('hqk,kd->qhd', weight_b.astype(jnp.float32), vals_all.astype(jnp.float32))
    result = summed / jnp.transpose(total)[:, :, None]
    return result.astype(jnp.bfloat16).reshape(nq, -1)


def reference(queries, keys, values, basis, picks):
    seq = NBLK * H
    sources = NBLK // 2
    q_rot = jnp.einsum('shd,de->she', queries.reshape(seq, HQ, HD).astype(jnp.float32), basis.astype(jnp.float32)).astype(jnp.bfloat16)
    kv_rows = jnp.concatenate([keys, values], axis=1)
    offsets = jnp.arange(KB, dtype=jnp.int32)

    def one_block(block):
        start = block_start(block, H)
        prev_start = block_start(jnp.maximum(block - 1, 0), H)
        chosen_ids = picks[block]
        index = jnp.arange(sources, dtype=jnp.int32)[:, None] * (2 * H) + jnp.maximum(chosen_ids, 0)[:, None] * KB + offsets[None, :]
        picked = jnp.take(kv_rows, index.reshape(-1).astype(jnp.int32), axis=0)
        ok_pick = jnp.repeat(chosen_ids >= 0, KB)
        before = lax.dynamic_slice_in_dim(kv_rows, prev_start, H, 0)
        ok_before = jnp.broadcast_to(block >= 1, (H,))
        chosen = jnp.concatenate([picked, before], axis=0)
        chosen_ok = jnp.concatenate([ok_pick, ok_before], axis=0)
        own = lax.dynamic_slice_in_dim(kv_rows, start, H, 0)
        q_block = lax.dynamic_slice_in_dim(q_rot, start, H, 0)
        return attend(q_block, chosen, chosen_ok, own)

    blocks = lax.map(one_block, jnp.arange(NBLK, dtype=jnp.int32))
    stored = jnp.stack([blocks[:sources], blocks[sources:][::-1]], axis=1)
    return stored.reshape(seq, HQ * HD)
```

```python
import functools
import math

import jax
import jax.numpy as jnp
from jax import lax
from jax.experimental import pallas as pl
from jax.experimental.pallas import tpu as pltpu
from jax.sharding import PartitionSpec as P

KB = 32
MESH = pl.DeviceIdType.MESH
F32 = jnp.float32
BF16 = jnp.bfloat16


def kernel(
    count, heads, dim, half,
    q_ref, ksub_ref, vsub_ref, basis_ref, picks_ref, out_ref,
    send, recv, prev, q_rot, top, acc, send_sem, recv_sem, prev_send, prev_recv,
):
    me = lax.axis_index("pb")
    rows = heads * half
    group = min(8, count)
    k_ref = ksub_ref.reshape(2 * half, dim)
    v_ref = vsub_ref.reshape(2 * half, dim)
    scale = dim ** (-0.5) * math.log2(math.e)

    def peer(i):
        return lax.rem(me + i, count)

    barrier = pltpu.get_barrier_semaphore()

    @pl.loop(1, count)
    def _(i):
        pl.semaphore_signal(barrier, inc=1, device_id={"pb": peer(i)}, device_id_type=MESH)


    @pl.loop(1, count)
    def _(i):
        d = peer(i)
        late = jnp.maximum(picks_ref[2 * count - 1 - d, me], 0)
        send[d, 1, 0] = ksub_ref[late]
        send[d, 1, 1] = vsub_ref[late]

        @pl.when(d > me + 1)
        def _():
            early = jnp.maximum(picks_ref[d, me], 0)
            send[d, 0, 0] = ksub_ref[early]
            send[d, 0, 1] = vsub_ref[early]

    own = jnp.maximum(picks_ref[2 * count - 1 - me, me], 0)
    recv[1, 0, me] = ksub_ref[own]
    recv[1, 1, me] = vsub_ref[own]

    @pl.loop(0, count)
    def _(s):
        @pl.when(s >= me - 1)
        def _():
            recv[0, 0, s] = jnp.zeros((KB, dim), BF16)
            recv[0, 1, s] = jnp.zeros((KB, dim), BF16)

    @pl.when(me == 0)
    def _():
        prev[0] = jnp.zeros((2, half, dim), BF16)

    @pl.when(me == count - 1)
    def _():
        prev[1, 0] = k_ref[:half, :]
        prev[1, 1] = v_ref[:half, :]

    pl.semaphore_wait(barrier, count - 1)

    def both(s, d):
        return pltpu.make_async_remote_copy(
            src_ref=send.at[d], dst_ref=recv.at[:, :, s], send_sem=send_sem.at[d],
            recv_sem=recv_sem.at[s], device_id={"pb": d}, device_id_type=MESH)

    def single(s, d):
        return pltpu.make_async_remote_copy(
            src_ref=send.at[d, 1], dst_ref=recv.at[1, :, s], send_sem=send_sem.at[d],
            recv_sem=recv_sem.at[s], device_id={"pb": d}, device_id_type=MESH)

    def neighbour(which, part, d):
        ref = (k_ref, v_ref)[part]
        return pltpu.make_async_remote_copy(
            src_ref=ref.at[pl.ds(which * half, half)], dst_ref=prev.at[which, part],
            send_sem=prev_send.at[which, part], recv_sem=prev_recv.at[which, part],
            device_id={"pb": d}, device_id_type=MESH)

    has_next = me < count - 1
    has_before = me > 0

    @pl.when(has_next)
    def _():
        neighbour(0, 0, me + 1).start()
        neighbour(0, 1, me + 1).start()

    @pl.when(has_before)
    def _():
        neighbour(1, 0, me - 1).start()
        neighbour(1, 1, me - 1).start()

    @pl.loop(1, count)
    def _(i):
        d = peer(i)

        @pl.when(d > me + 1)
        def _():
            both(me, d).start()

        @pl.when(d <= me + 1)
        def _():
            single(me, d).start()

    basis = basis_ref[...]
    for w in range(2):
        for h in range(heads):
            q = q_ref[w * half:(w + 1) * half, h * dim:(h + 1) * dim]
            q_rot[w, h * half:(h + 1) * half, :] = jnp.dot(
                q, basis, preferred_element_type=F32).astype(BF16)

    @pl.when(has_before)
    def _():
        neighbour(0, 0, me - 1).wait_recv()
        neighbour(0, 1, me - 1).wait_recv()

    @pl.when(has_next)
    def _():
        neighbour(1, 0, me + 1).wait_recv()
        neighbour(1, 1, me + 1).wait_recv()

    ones_own = jnp.ones((2 * half, dim), BF16)
    row = lax.broadcasted_iota(jnp.int32, (half, 2 * half), 0)
    col = lax.broadcasted_iota(jnp.int32, (half, 2 * half), 1)
    for w in range(2):
        keys = jnp.concatenate([k_ref[w * half:(w + 1) * half, :], prev[w, 0]], axis=0)
        vals = jnp.concatenate([v_ref[w * half:(w + 1) * half, :], prev[w, 1]], axis=0)
        vals = jnp.concatenate([vals, ones_own], axis=1)
        usable = col <= row
        if w == 0:
            usable = usable | ((col >= half) & (me >= 1))
        else:
            usable = usable | (col >= half)
        bias = jnp.where(usable, F32(0), F32(-1e30))
        for h in range(heads):
            at = slice(h * half, (h + 1) * half)
            s = lax.dot_general(q_rot[w, at, :], keys, (((1,), (1,)), ((), ())),
                                preferred_element_type=F32)
            s = jnp.where(usable, s * scale, F32(-1e30))
            m = jnp.max(s, axis=-1, keepdims=True)
            p = jnp.exp2((s - m).astype(BF16))
            acc[w, at, :] = jnp.dot(p, vals, preferred_element_type=F32)
            top[w, at, :] = jnp.broadcast_to(m, (half, dim))

    ones_far = jnp.ones((group * KB, dim), BF16)
    far_col = lax.broadcasted_iota(jnp.int32, (1, group * KB), 1)

    @pl.loop(0, count // group)
    def _(g):
        @pl.loop(g * group, (g + 1) * group)
        def _(s):
            @pl.when((s < me - 1) & (s != me))
            def _():
                both(s, me).wait_recv()

            @pl.when((s >= me - 1) & (s != me))
            def _():
                single(s, me).wait_recv()

        for w in range(2):
            limit = (me - 1) * KB if w == 0 else jnp.where(me == count - 1, (count - 1) * KB, count * KB)
            usable = far_col + g * (group * KB) < limit
            keys = recv[w, 0, pl.ds(g * group, group)].reshape(group * KB, dim)
            vals = recv[w, 1, pl.ds(g * group, group)].reshape(group * KB, dim)
            vals = jnp.concatenate([vals, ones_far], axis=1)
            for h in range(heads):
                at = slice(h * half, (h + 1) * half)
                s = lax.dot_general(q_rot[w, at, :], keys, (((1,), (1,)), ((), ())),
                                    preferred_element_type=F32)
                s = jnp.where(usable, s * scale, F32(-1e30))
                old = top[w, at, :]
                m = jnp.maximum(old, jnp.max(s, axis=-1, keepdims=True))
                p = jnp.exp2((s - m[:, :1]).astype(BF16))
                keep = jnp.exp2(old - m)
                keep = jnp.concatenate([keep, keep], axis=1)
                acc[w, at, :] = acc[w, at, :] * keep + jnp.dot(p, vals, preferred_element_type=F32)
                top[w, at, :] = m

    for w in range(2):
        for h in range(heads):
            at = slice(h * half, (h + 1) * half)
            out_ref[w * half:(w + 1) * half, h * dim:(h + 1) * dim] = (
                acc[w, at, :dim] / acc[w, at, dim:]).astype(BF16)

    @pl.when(has_next)
    def _():
        neighbour(0, 0, me + 1).wait_send()
        neighbour(0, 1, me + 1).wait_send()

    @pl.when(has_before)
    def _():
        neighbour(1, 0, me - 1).wait_send()
        neighbour(1, 1, me - 1).wait_send()

    @pl.loop(1, count)
    def _(i):
        d = peer(i)

        @pl.when(d > me + 1)
        def _():
            both(me, d).wait_send()

        @pl.when(d <= me + 1)
        def _():
            single(me, d).wait_send()


def per_device(queries, keys, values, basis, picks):
    half = queries.shape[0] // 2
    dim = basis.shape[0]
    heads = queries.shape[1] // dim
    count = lax.axis_size("pb")
    rows = heads * half
    vmem = pl.BlockSpec(memory_space=pltpu.VMEM)
    return pl.pallas_call(
        functools.partial(kernel, count, heads, dim, half),
        out_shape=jax.ShapeDtypeStruct(queries.shape, BF16),
        in_specs=[vmem] * 4 + [pl.BlockSpec(memory_space=pltpu.SMEM)],
        out_specs=vmem,
        scratch_shapes=[
            pltpu.VMEM((count, 2, 2, KB, dim), BF16),
            pltpu.VMEM((2, 2, count, KB, dim), BF16),
            pltpu.VMEM((2, 2, half, dim), BF16),
            pltpu.VMEM((2, rows, dim), BF16),
            pltpu.VMEM((2, rows, dim), F32),
            pltpu.VMEM((2, rows, 2 * dim), F32),
            pltpu.SemaphoreType.DMA((count,)),
            pltpu.SemaphoreType.DMA((count,)),
            pltpu.SemaphoreType.DMA((2, 2)),
            pltpu.SemaphoreType.DMA((2, 2)),
        ],
        compiler_params=pltpu.CompilerParams(collective_id=0, has_side_effects=True),
        name="exchange_attend",
    )(queries, keys.reshape(-1, KB, dim), values.reshape(-1, KB, dim), basis, picks)


def solution(mesh):
    in_specs = (P("pb", "grp"), P("pb", "grp"), P("pb", "grp"), P("grp", None), P("grp", None))
    out_specs = P("pb", "grp")
    return jax.shard_map(
        per_device, mesh=mesh, in_specs=in_specs, out_specs=out_specs, check_vma=False
    )
```

```python
import functools
import math

import jax
import jax.numpy as jnp
from jax import lax
from jax.experimental import pallas as pl
from jax.experimental.pallas import tpu as pltpu
from jax.sharding import PartitionSpec as P

KB = 32
MESH = pl.DeviceIdType.MESH
F32 = jnp.float32
BF16 = jnp.bfloat16


def kernel(
    count, heads, dim, half,
    q_hbm, k_hbm, v_hbm, basis_hbm, picks_hbm, out_ref,
    q_ref, ksub_ref, vsub_ref, basis_ref, picks_ref,
    send, recv, prev, q_rot, top, acc, send_sem, recv_sem, prev_send, prev_recv, load_sem,
):
    me = lax.axis_index("pb")
    rows = heads * half
    group = min(16, count)
    span = heads // 2 * half
    k_ref = ksub_ref.reshape(2 * half, dim)
    v_ref = vsub_ref.reshape(2 * half, dim)
    scale = dim ** (-0.5) * math.log2(math.e)

    def peer(i):
        return lax.rem(me + i, count)

    barrier = pltpu.get_barrier_semaphore()

    @pl.loop(1, count)
    def _(i):
        pl.semaphore_signal(barrier, inc=1, device_id={"pb": peer(i)}, device_id_type=MESH)


    pairs = ((picks_hbm, picks_ref), (k_hbm, ksub_ref), (v_hbm, vsub_ref),
             (q_hbm, q_ref), (basis_hbm, basis_ref))
    loads = [pltpu.make_async_copy(a, b, load_sem.at[i]) for i, (a, b) in enumerate(pairs)]
    for load in loads:
        load.start()
    for load in loads[:3]:
        load.wait()

    @pl.loop(1, count)
    def _(i):
        d = peer(i)
        late = jnp.maximum(picks_ref[me, 2 * count - 1 - d], 0)
        send[d, 1, 0] = ksub_ref[late]
        send[d, 1, 1] = vsub_ref[late]

        @pl.when(d > me + 1)
        def _():
            early = jnp.maximum(picks_ref[me, d], 0)
            send[d, 0, 0] = ksub_ref[early]
            send[d, 0, 1] = vsub_ref[early]

    own = jnp.maximum(picks_ref[me, 2 * count - 1 - me], 0)
    recv[1, 0, me] = ksub_ref[own]
    recv[1, 1, me] = vsub_ref[own]

    @pl.loop(0, count)
    def _(s):
        @pl.when(s >= me - 1)
        def _():
            recv[0, 0, s] = jnp.zeros((KB, dim), BF16)
            recv[0, 1, s] = jnp.zeros((KB, dim), BF16)

    @pl.when(me == 0)
    def _():
        prev[0] = jnp.zeros((2, half, dim), BF16)

    @pl.when(me == count - 1)
    def _():
        prev[1, 0] = k_ref[:half, :]
        prev[1, 1] = v_ref[:half, :]

    pl.semaphore_wait(barrier, count - 1)

    def both(s, d):
        return pltpu.make_async_remote_copy(
            src_ref=send.at[d], dst_ref=recv.at[:, :, s], send_sem=send_sem.at[d],
            recv_sem=recv_sem.at[s], device_id={"pb": d}, device_id_type=MESH)

    def single(s, d):
        return pltpu.make_async_remote_copy(
            src_ref=send.at[d, 1], dst_ref=recv.at[1, :, s], send_sem=send_sem.at[d],
            recv_sem=recv_sem.at[s], device_id={"pb": d}, device_id_type=MESH)

    def neighbour(which, part, d):
        ref = (k_ref, v_ref)[part]
        return pltpu.make_async_remote_copy(
            src_ref=ref.at[pl.ds(which * half, half)], dst_ref=prev.at[which, part],
            send_sem=prev_send.at[which, part], recv_sem=prev_recv.at[which, part],
            device_id={"pb": d}, device_id_type=MESH)

    has_next = me < count - 1
    has_before = me > 0

    @pl.when(has_next)
    def _():
        neighbour(0, 0, me + 1).start()
        neighbour(0, 1, me + 1).start()

    @pl.when(has_before)
    def _():
        neighbour(1, 0, me - 1).start()
        neighbour(1, 1, me - 1).start()

    @pl.loop(1, count)
    def _(i):
        d = peer(i)

        @pl.when(d > me + 1)
        def _():
            both(me, d).start()

        @pl.when(d <= me + 1)
        def _():
            single(me, d).start()

    loads[3].wait()
    loads[4].wait()
    basis = basis_ref[...]
    for w in range(2):
        for h in range(heads):
            q = q_ref[w * half:(w + 1) * half, h * dim:(h + 1) * dim]
            q_rot[w, h * half:(h + 1) * half, :] = jnp.dot(
                q, basis, preferred_element_type=F32).astype(BF16)

    @pl.when(has_before)
    def _():
        neighbour(0, 0, me - 1).wait_recv()
        neighbour(0, 1, me - 1).wait_recv()

    @pl.when(has_next)
    def _():
        neighbour(1, 0, me + 1).wait_recv()
        neighbour(1, 1, me + 1).wait_recv()

    ones_own = jnp.ones((2 * half, dim), BF16)
    row = lax.broadcasted_iota(jnp.int32, (half, 2 * half), 0)
    col = lax.broadcasted_iota(jnp.int32, (half, 2 * half), 1)
    for w in range(2):
        keys = jnp.concatenate([k_ref[w * half:(w + 1) * half, :], prev[w, 0]], axis=0)
        vals = jnp.concatenate([v_ref[w * half:(w + 1) * half, :], prev[w, 1]], axis=0)
        vals = jnp.concatenate([vals, ones_own], axis=1)
        usable = col <= row
        if w == 0:
            usable = usable | ((col >= half) & (me >= 1))
        else:
            usable = usable | (col >= half)
        for part in range(2):
            at = slice(part * span, (part + 1) * span)
            s = lax.dot_general(q_rot[w, at, :], keys, (((1,), (1,)), ((), ())),
                                preferred_element_type=F32)
            s = jnp.where(usable[None], s.reshape(-1, half, 2 * half), F32(-1e30)).reshape(span, -1)
            m = jnp.max(s, axis=-1, keepdims=True)
            p = jnp.exp2(((s - m) * scale).astype(BF16))
            acc[w, at, :] = jnp.dot(p, vals, preferred_element_type=F32)
            top[w, at, :] = jnp.broadcast_to(m, (span, dim))

    ones_far = jnp.ones((group * KB, dim), BF16)
    far_col = lax.broadcasted_iota(jnp.int32, (1, group * KB), 1)

    @pl.loop(0, count // group)
    def _(g):
        @pl.loop(g * group, (g + 1) * group)
        def _(s):
            @pl.when((s < me - 1) & (s != me))
            def _():
                both(s, me).wait_recv()

            @pl.when((s >= me - 1) & (s != me))
            def _():
                single(s, me).wait_recv()

        for w in range(2):
            limit = (me - 1) * KB if w == 0 else jnp.where(me == count - 1, (count - 1) * KB, count * KB)
            usable = far_col + g * (group * KB) < limit
            keys = recv[w, 0, pl.ds(g * group, group)].reshape(group * KB, dim)
            vals = recv[w, 1, pl.ds(g * group, group)].reshape(group * KB, dim)
            vals = jnp.concatenate([vals, ones_far], axis=1)
            for part in range(2):
                at = slice(part * span, (part + 1) * span)
                s = lax.dot_general(q_rot[w, at, :], keys, (((1,), (1,)), ((), ())),
                                    preferred_element_type=F32)
                s = jnp.where(usable, s, F32(-1e30))
                old = top[w, at, :]
                m = jnp.maximum(old, jnp.max(s, axis=-1, keepdims=True))
                p = jnp.exp2(((s - m[:, :1]) * scale).astype(BF16))
                keep = jnp.exp2((old - m) * scale)
                keep = jnp.concatenate([keep, keep], axis=1)
                acc[w, at, :] = acc[w, at, :] * keep + jnp.dot(p, vals, preferred_element_type=F32)
                top[w, at, :] = m

    for w in range(2):
        for h in range(heads):
            at = slice(h * half, (h + 1) * half)
            out_ref[w * half:(w + 1) * half, h * dim:(h + 1) * dim] = (
                acc[w, at, :dim] / acc[w, at, dim:]).astype(BF16)

    @pl.when(has_next)
    def _():
        neighbour(0, 0, me + 1).wait_send()
        neighbour(0, 1, me + 1).wait_send()

    @pl.when(has_before)
    def _():
        neighbour(1, 0, me - 1).wait_send()
        neighbour(1, 1, me - 1).wait_send()

    @pl.loop(1, count)
    def _(i):
        d = peer(i)

        @pl.when(d > me + 1)
        def _():
            both(me, d).wait_send()

        @pl.when(d <= me + 1)
        def _():
            single(me, d).wait_send()


def per_device(queries, keys, values, basis, picks):
    half = queries.shape[0] // 2
    dim = basis.shape[0]
    heads = queries.shape[1] // dim
    count = lax.axis_size("pb")
    rows = heads * half
    vmem = pl.BlockSpec(memory_space=pltpu.VMEM)
    made = pl.pallas_call(
        functools.partial(kernel, count, heads, dim, half),
        out_shape=pltpu.VMEM(queries.shape, BF16),
        in_specs=[pl.BlockSpec(memory_space=pl.ANY)] * 5,
        out_specs=vmem,
        scratch_shapes=[
            pltpu.VMEM(queries.shape, BF16),
            pltpu.VMEM((2 * half // KB, KB, dim), BF16),
            pltpu.VMEM((2 * half // KB, KB, dim), BF16),
            pltpu.VMEM(basis.shape, BF16),
            pltpu.SMEM(picks.shape[::-1], jnp.int32),
            pltpu.VMEM((count, 2, 2, KB, dim), BF16),
            pltpu.VMEM((2, 2, count, KB, dim), BF16),
            pltpu.VMEM((2, 2, half, dim), BF16),
            pltpu.VMEM((2, rows, dim), BF16),
            pltpu.VMEM((2, rows, dim), F32),
            pltpu.VMEM((2, rows, 2 * dim), F32),
            pltpu.SemaphoreType.DMA((count,)),
            pltpu.SemaphoreType.DMA((count,)),
            pltpu.SemaphoreType.DMA((2, 2)),
            pltpu.SemaphoreType.DMA((2, 2)),
            pltpu.SemaphoreType.DMA((5,)),
        ],
        compiler_params=pltpu.CompilerParams(collective_id=0, has_side_effects=True),
        name="exchange_attend",
    )(queries, keys.reshape(-1, KB, dim), values.reshape(-1, KB, dim), basis, picks.T)
    return pl.pallas_call(
        place, out_shape=jax.ShapeDtypeStruct(queries.shape, BF16),
        in_specs=[vmem], out_specs=vmem, name="place_result")(pltpu.with_memory_space_constraint(made, pltpu.VMEM))


def place(a_ref, o_ref):
    o_ref[...] = a_ref[...]


def solution(mesh):
    in_specs = (P("pb", "grp"), P("pb", "grp"), P("pb", "grp"), P("grp", None), P("grp", None))
    out_specs = P("pb", "grp")
    return jax.shard_map(
        per_device, mesh=mesh, in_specs=in_specs, out_specs=out_specs, check_vma=False
    )
```

```python
import functools
import math

import jax
import jax.numpy as jnp
from jax import lax
from jax.experimental import pallas as pl
from jax.experimental.pallas import tpu as pltpu
from jax.sharding import PartitionSpec as P

KB = 32
GROUP = 4
MESH = pl.DeviceIdType.MESH
F32 = jnp.float32
BF16 = jnp.bfloat16


def kernel(
    count, heads, dim, half,
    q_hbm, k_hbm, v_hbm, basis_hbm, picks_hbm, out_ref,
    q_ref, kv_ref, basis_ref, picks_ref,
    send, recv, prev, q_rot, top, acc, send_sem, recv_sem, prev_send, prev_recv, load_sem,
    forward, forward_send, raw_send, raw_recv, *raw,
):
    me = lax.axis_index("pb")
    group = min(16, count)
    span = heads // 2 * half
    planes = count // GROUP
    subs = half // KB
    plane, column = me // GROUP, lax.rem(me, GROUP)
    scale = dim ** (-0.5) * math.log2(math.e)

    def peer(i):
        return lax.rem(me + i, count)

    barrier = pltpu.get_barrier_semaphore()

    @pl.loop(1, count)
    def _(i):
        pl.semaphore_signal(barrier, inc=1, device_id={"pb": peer(i)}, device_id_type=MESH)


    pairs = ((picks_hbm, picks_ref), (k_hbm, kv_ref.at[0]), (v_hbm, kv_ref.at[1]),
             (q_hbm, q_ref), (basis_hbm, basis_ref))
    loads = [pltpu.make_async_copy(a, b, load_sem.at[i]) for i, (a, b) in enumerate(pairs)]
    for load in loads:
        load.start()
    for load in loads[:3]:
        load.wait()

    pl.semaphore_wait(barrier, count - 1)

    def whole(step, d):
        return pltpu.make_async_remote_copy(
            src_ref=kv_ref.at[:, pl.ds(0, subs)], dst_ref=raw[step - 1],
            send_sem=raw_send.at[step - 1], recv_sem=raw_recv.at[step - 1],
            device_id={"pb": d}, device_id_type=MESH)

    def passed(step, i, s, d):
        return pltpu.make_async_remote_copy(
            src_ref=forward.at[step - 1, i], dst_ref=recv.at[:, :, s],
            send_sem=forward_send.at[step - 1, i], recv_sem=recv_sem.at[s],
            device_id={"pb": d}, device_id_type=MESH)

    def passed_single(step, i, s, d):
        return pltpu.make_async_remote_copy(
            src_ref=forward.at[step - 1, i, 1], dst_ref=recv.at[1, :, s],
            send_sem=forward_send.at[step - 1, i], recv_sem=recv_sem.at[s],
            device_id={"pb": d}, device_id_type=MESH)

    def both(s, d):
        return pltpu.make_async_remote_copy(
            src_ref=send.at[d], dst_ref=recv.at[:, :, s], send_sem=send_sem.at[d],
            recv_sem=recv_sem.at[s], device_id={"pb": d}, device_id_type=MESH)

    def single(s, d):
        return pltpu.make_async_remote_copy(
            src_ref=send.at[d, 1], dst_ref=recv.at[1, :, s], send_sem=send_sem.at[d],
            recv_sem=recv_sem.at[s], device_id={"pb": d}, device_id_type=MESH)

    def neighbour(which, d):
        return pltpu.make_async_remote_copy(
            src_ref=kv_ref.at[:, pl.ds(which * subs, subs)], dst_ref=prev.at[which],
            send_sem=prev_send.at[which], recv_sem=prev_recv.at[which],
            device_id={"pb": d}, device_id_type=MESH)

    has_next = me < count - 1
    has_before = me > 0

    for step in range(planes - 1, 0, -1):
        @pl.when(plane + step < planes)
        def _():
            whole(step, me + step * GROUP).start()

    @pl.when(has_next)
    def _():
        neighbour(0, me + 1).start()

    @pl.when(has_before)
    def _():
        neighbour(1, me - 1).start()

    @pl.loop(1, count)
    def _(i):
        d = peer(i)

        @pl.when(d // GROUP <= plane)
        def _():
            late = jnp.maximum(picks_ref[me, 2 * count - 1 - d], 0)
            send[d, 1, 0] = kv_ref[0, late]
            send[d, 1, 1] = kv_ref[1, late]

            @pl.when(d > me + 1)
            def _():
                early = jnp.maximum(picks_ref[me, d], 0)
                send[d, 0, 0] = kv_ref[0, early]
                send[d, 0, 1] = kv_ref[1, early]

    own = jnp.maximum(picks_ref[me, 2 * count - 1 - me], 0)
    recv[1, 0, me] = kv_ref[0, own]
    recv[1, 1, me] = kv_ref[1, own]

    @pl.loop(0, count)
    def _(s):
        @pl.when(s >= me - 1)
        def _():
            recv[0, 0, s] = jnp.zeros((KB, dim), BF16)
            recv[0, 1, s] = jnp.zeros((KB, dim), BF16)

    @pl.when(me == 0)
    def _():
        prev[0] = jnp.zeros((2, subs, KB, dim), BF16)

    @pl.when(me == count - 1)
    def _():
        prev[1] = kv_ref[:, :subs]

    @pl.loop(1, count)
    def _(i):
        d = peer(i)

        @pl.when(d > me + 1)
        def _():
            @pl.when(d // GROUP == plane)
            def _():
                both(me, d).start()

        @pl.when(d <= me + 1)
        def _():
            @pl.when(d // GROUP <= plane)
            def _():
                single(me, d).start()

    loads[3].wait()
    loads[4].wait()
    basis = basis_ref[...]
    for w in range(2):
        for h in range(heads):
            q = q_ref[w * half:(w + 1) * half, h * dim:(h + 1) * dim]
            q_rot[w, h * half:(h + 1) * half, :] = jnp.dot(
                q, basis, preferred_element_type=F32).astype(BF16)

    @pl.when(has_before)
    def _():
        neighbour(0, me - 1).wait_recv()

    @pl.when(has_next)
    def _():
        neighbour(1, me + 1).wait_recv()

    def relay(step):
        s = me - step * GROUP
        held = raw[step - 1]

        @pl.when(plane >= step)
        def _():
            whole(step, s).wait_recv()

            @pl.loop(1, GROUP)
            def _(i):
                d = plane * GROUP + lax.rem(column + i, GROUP)
                late = jnp.maximum(picks_ref[s, 2 * count - 1 - d], 0)
                early = jnp.maximum(picks_ref[s, d], 0)
                for part in range(2):
                    forward[step - 1, i, 0, part] = held[part, early]
                    forward[step - 1, i, 1, part] = held[part, late]

            late = jnp.maximum(picks_ref[s, 2 * count - 1 - me], 0)
            early = jnp.maximum(picks_ref[s, me], 0)
            for part in range(2):
                recv[0, part, s] = held[part, early]
                recv[1, part, s] = held[part, late]

            @pl.loop(1, GROUP)
            def _(i):
                d = plane * GROUP + lax.rem(column + i, GROUP)

                @pl.when(d > s + 1)
                def _():
                    passed(step, i, s, d).start()

                @pl.when(d <= s + 1)
                def _():
                    passed_single(step, i, s, d).start()

    ones_own = jnp.ones((2 * half, dim), BF16)
    row = lax.broadcasted_iota(jnp.int32, (half, 2 * half), 0)
    col = lax.broadcasted_iota(jnp.int32, (half, 2 * half), 1)
    for w in range(2):
        here = slice(w * subs, (w + 1) * subs)
        keys = jnp.concatenate([kv_ref[0, here], prev[w, 0]], axis=0).reshape(2 * half, dim)
        vals = jnp.concatenate([kv_ref[1, here], prev[w, 1]], axis=0).reshape(2 * half, dim)
        vals = jnp.concatenate([vals, ones_own], axis=1)
        usable = col <= row
        if w == 0:
            usable = usable | ((col >= half) & (me >= 1))
        else:
            usable = usable | (col >= half)
        for part in range(2):
            at = slice(part * span, (part + 1) * span)
            s = lax.dot_general(q_rot[w, at, :], keys, (((1,), (1,)), ((), ())),
                                preferred_element_type=F32)
            s = jnp.where(usable[None], s.reshape(-1, half, 2 * half), F32(-1e30)).reshape(span, -1)
            m = jnp.max(s, axis=-1, keepdims=True)
            p = jnp.exp2(((s - m) * scale).astype(BF16))
            acc[w, at, :] = jnp.dot(p, vals, preferred_element_type=F32)
            top[w, at, :] = jnp.broadcast_to(m, (span, dim))
        if w == 0 and planes > 1:
            relay(1)

    for step in range(2, planes):
        relay(step)

    ones_far = jnp.ones((group * KB, dim), BF16)
    far_col = lax.broadcasted_iota(jnp.int32, (1, group * KB), 1)

    @pl.loop(0, count // group)
    def _(g):
        @pl.loop(g * group, (g + 1) * group)
        def _(s):
            mine = (s < plane * GROUP) & (lax.rem(s, GROUP) == column)

            @pl.when((s < me - 1) & jnp.logical_not(mine))
            def _():
                both(s, me).wait_recv()

            @pl.when((s >= me - 1) & (s != me) & jnp.logical_not(mine))
            def _():
                single(s, me).wait_recv()

        for w in range(2):
            limit = (me - 1) * KB if w == 0 else jnp.where(me == count - 1, (count - 1) * KB, count * KB)
            usable = far_col + g * (group * KB) < limit
            keys = recv[w, 0, pl.ds(g * group, group)].reshape(group * KB, dim)
            vals = recv[w, 1, pl.ds(g * group, group)].reshape(group * KB, dim)
            vals = jnp.concatenate([vals, ones_far], axis=1)
            for part in range(2):
                at = slice(part * span, (part + 1) * span)
                s = lax.dot_general(q_rot[w, at, :], keys, (((1,), (1,)), ((), ())),
                                    preferred_element_type=F32)
                s = jnp.where(usable, s, F32(-1e30))
                old = top[w, at, :]
                m = jnp.maximum(old, jnp.max(s, axis=-1, keepdims=True))
                p = jnp.exp2(((s - m[:, :1]) * scale).astype(BF16))
                keep = jnp.exp2((old - m) * scale)
                keep = jnp.concatenate([keep, keep], axis=1)
                acc[w, at, :] = acc[w, at, :] * keep + jnp.dot(p, vals, preferred_element_type=F32)
                top[w, at, :] = m

    for w in range(2):
        for h in range(heads):
            at = slice(h * half, (h + 1) * half)
            out_ref[w * half:(w + 1) * half, h * dim:(h + 1) * dim] = (
                acc[w, at, :dim] / acc[w, at, dim:]).astype(BF16)

    @pl.when(has_next)
    def _():
        neighbour(0, me + 1).wait_send()

    @pl.when(has_before)
    def _():
        neighbour(1, me - 1).wait_send()

    for step in range(1, planes):
        @pl.when(plane + step < planes)
        def _():
            whole(step, me + step * GROUP).wait_send()

        @pl.when(plane >= step)
        def _():
            s = me - step * GROUP

            @pl.loop(1, GROUP)
            def _(i):
                d = plane * GROUP + lax.rem(column + i, GROUP)

                @pl.when(d > s + 1)
                def _():
                    passed(step, i, s, d).wait_send()

                @pl.when(d <= s + 1)
                def _():
                    passed_single(step, i, s, d).wait_send()

    @pl.loop(1, count)
    def _(i):
        d = peer(i)

        @pl.when(d > me + 1)
        def _():
            @pl.when(d // GROUP == plane)
            def _():
                both(me, d).wait_send()

        @pl.when(d <= me + 1)
        def _():
            @pl.when(d // GROUP <= plane)
            def _():
                single(me, d).wait_send()


def per_device(queries, keys, values, basis, picks):
    half = queries.shape[0] // 2
    dim = basis.shape[0]
    heads = queries.shape[1] // dim
    count = lax.axis_size("pb")
    rows = heads * half
    planes = count // GROUP
    vmem = pl.BlockSpec(memory_space=pltpu.VMEM)
    made = pl.pallas_call(
        functools.partial(kernel, count, heads, dim, half),
        out_shape=pltpu.VMEM(queries.shape, BF16),
        in_specs=[pl.BlockSpec(memory_space=pl.ANY)] * 5,
        out_specs=vmem,
        scratch_shapes=[
            pltpu.VMEM(queries.shape, BF16),
            pltpu.VMEM((2, 2 * half // KB, KB, dim), BF16),
            pltpu.VMEM(basis.shape, BF16),
            pltpu.SMEM(picks.shape[::-1], jnp.int32),
            pltpu.VMEM((count, 2, 2, KB, dim), BF16),
            pltpu.VMEM((2, 2, count, KB, dim), BF16),
            pltpu.VMEM((2, 2, half // KB, KB, dim), BF16),
            pltpu.VMEM((2, rows, dim), BF16),
            pltpu.VMEM((2, rows, dim), F32),
            pltpu.VMEM((2, rows, 2 * dim), F32),
            pltpu.SemaphoreType.DMA((count,)),
            pltpu.SemaphoreType.DMA((count,)),
            pltpu.SemaphoreType.DMA((2,)),
            pltpu.SemaphoreType.DMA((2,)),
            pltpu.SemaphoreType.DMA((5,)),
            pltpu.VMEM((planes - 1, GROUP, 2, 2, KB, dim), BF16),
            pltpu.SemaphoreType.DMA((planes - 1, GROUP)),
            pltpu.SemaphoreType.DMA((planes - 1,)),
            pltpu.SemaphoreType.DMA((planes - 1,)),
            *[pltpu.VMEM((2, half // KB, KB, dim), BF16) for _ in range(planes - 1)],
        ],
        compiler_params=pltpu.CompilerParams(collective_id=0, has_side_effects=True),
        name="exchange_attend",
    )(queries, keys.reshape(-1, KB, dim), values.reshape(-1, KB, dim), basis, picks.T)
    return pl.pallas_call(
        place, out_shape=jax.ShapeDtypeStruct(queries.shape, BF16),
        in_specs=[vmem], out_specs=vmem, name="place_result")(pltpu.with_memory_space_constraint(made, pltpu.VMEM))


def place(a_ref, o_ref):
    o_ref[...] = a_ref[...]


def solution(mesh):
    in_specs = (P("pb", "grp"), P("pb", "grp"), P("pb", "grp"), P("grp", None), P("grp", None))
    out_specs = P("pb", "grp")
    return jax.shard_map(
        per_device, mesh=mesh, in_specs=in_specs, out_specs=out_specs, check_vma=False
    )
```

```python
import functools
import math

import jax
import jax.numpy as jnp
from jax import lax
from jax.experimental import pallas as pl
from jax.experimental.pallas import tpu as pltpu
from jax.sharding import PartitionSpec as P

KB = 32
GROUP = 4
DIRECT = 1
MESH = pl.DeviceIdType.MESH
F32 = jnp.float32
BF16 = jnp.bfloat16


def kernel(
    count, heads, dim, half,
    q_hbm, k_hbm, v_hbm, basis_hbm, picks_hbm, out_ref,
    q_ref, kv_ref, basis_ref, picks_ref,
    send, recv, prev, q_rot, top, acc, send_sem, recv_sem, prev_send, prev_recv, load_sem,
    forward, forward_send, raw_send, raw_recv, *raw,
):
    me = lax.axis_index("pb")
    group = min(16, count)
    span = heads // 2 * half
    planes = count // GROUP
    subs = half // KB
    plane, column = me // GROUP, lax.rem(me, GROUP)
    scale = dim ** (-0.5) * math.log2(math.e)

    def peer(i):
        return lax.rem(me + i, count)

    barrier = pltpu.get_barrier_semaphore()

    @pl.loop(1, count)
    def _(i):
        pl.semaphore_signal(barrier, inc=1, device_id={"pb": peer(i)}, device_id_type=MESH)


    pairs = ((picks_hbm, picks_ref), (k_hbm, kv_ref.at[0]), (v_hbm, kv_ref.at[1]),
             (q_hbm, q_ref), (basis_hbm, basis_ref))
    loads = [pltpu.make_async_copy(a, b, load_sem.at[i]) for i, (a, b) in enumerate(pairs)]
    for load in loads:
        load.start()
    for load in loads[:3]:
        load.wait()

    pl.semaphore_wait(barrier, count - 1)

    def whole(step, d):
        return pltpu.make_async_remote_copy(
            src_ref=kv_ref.at[:, pl.ds(0, subs)], dst_ref=raw[step - 1],
            send_sem=raw_send.at[step - 1], recv_sem=raw_recv.at[step - 1],
            device_id={"pb": d}, device_id_type=MESH)

    def passed(step, i, s, d):
        return pltpu.make_async_remote_copy(
            src_ref=forward.at[step - 1, i], dst_ref=recv.at[:, :, s],
            send_sem=forward_send.at[step - 1, i], recv_sem=recv_sem.at[s],
            device_id={"pb": d}, device_id_type=MESH)

    def passed_single(step, i, s, d):
        return pltpu.make_async_remote_copy(
            src_ref=forward.at[step - 1, i, 1], dst_ref=recv.at[1, :, s],
            send_sem=forward_send.at[step - 1, i], recv_sem=recv_sem.at[s],
            device_id={"pb": d}, device_id_type=MESH)

    def both(s, d):
        return pltpu.make_async_remote_copy(
            src_ref=send.at[d], dst_ref=recv.at[:, :, s], send_sem=send_sem.at[d],
            recv_sem=recv_sem.at[s], device_id={"pb": d}, device_id_type=MESH)

    def single(s, d):
        return pltpu.make_async_remote_copy(
            src_ref=send.at[d, 1], dst_ref=recv.at[1, :, s], send_sem=send_sem.at[d],
            recv_sem=recv_sem.at[s], device_id={"pb": d}, device_id_type=MESH)

    def neighbour(which, d):
        return pltpu.make_async_remote_copy(
            src_ref=kv_ref.at[:, pl.ds(which * subs, subs)], dst_ref=prev.at[which],
            send_sem=prev_send.at[which], recv_sem=prev_recv.at[which],
            device_id={"pb": d}, device_id_type=MESH)

    has_next = me < count - 1
    has_before = me > 0

    for step in range(planes - 1, DIRECT, -1):
        @pl.when(plane + step < planes)
        def _():
            whole(step, me + step * GROUP).start()

    @pl.when(has_next)
    def _():
        neighbour(0, me + 1).start()

    @pl.when(has_before)
    def _():
        neighbour(1, me - 1).start()

    @pl.loop(1, count)
    def _(i):
        d = peer(i)

        @pl.when(d // GROUP <= plane + DIRECT)
        def _():
            late = jnp.maximum(picks_ref[me, 2 * count - 1 - d], 0)
            send[d, 1, 0] = kv_ref[0, late]
            send[d, 1, 1] = kv_ref[1, late]

            @pl.when(d > me + 1)
            def _():
                early = jnp.maximum(picks_ref[me, d], 0)
                send[d, 0, 0] = kv_ref[0, early]
                send[d, 0, 1] = kv_ref[1, early]

    own = jnp.maximum(picks_ref[me, 2 * count - 1 - me], 0)
    recv[1, 0, me] = kv_ref[0, own]
    recv[1, 1, me] = kv_ref[1, own]

    @pl.loop(0, count)
    def _(s):
        @pl.when(s >= me - 1)
        def _():
            recv[0, 0, s] = jnp.zeros((KB, dim), BF16)
            recv[0, 1, s] = jnp.zeros((KB, dim), BF16)

    @pl.when(me == 0)
    def _():
        prev[0] = jnp.zeros((2, subs, KB, dim), BF16)

    @pl.when(me == count - 1)
    def _():
        prev[1] = kv_ref[:, :subs]

    @pl.loop(1, count)
    def _(i):
        d = peer(i)

        @pl.when(d > me + 1)
        def _():
            @pl.when(d // GROUP <= plane + DIRECT)
            def _():
                both(me, d).start()

        @pl.when(d <= me + 1)
        def _():
            @pl.when(d // GROUP <= plane + DIRECT)
            def _():
                single(me, d).start()

    loads[3].wait()
    loads[4].wait()
    basis = basis_ref[...]
    for w in range(2):
        for h in range(heads):
            q = q_ref[w * half:(w + 1) * half, h * dim:(h + 1) * dim]
            q_rot[w, h * half:(h + 1) * half, :] = jnp.dot(
                q, basis, preferred_element_type=F32).astype(BF16)

    @pl.when(has_before)
    def _():
        neighbour(0, me - 1).wait_recv()

    @pl.when(has_next)
    def _():
        neighbour(1, me + 1).wait_recv()

    def relay(step):
        s = me - step * GROUP
        held = raw[step - 1]

        @pl.when(plane >= step)
        def _():
            whole(step, s).wait_recv()

            @pl.loop(1, GROUP)
            def _(i):
                d = plane * GROUP + lax.rem(column + i, GROUP)
                late = jnp.maximum(picks_ref[s, 2 * count - 1 - d], 0)
                early = jnp.maximum(picks_ref[s, d], 0)
                for part in range(2):
                    forward[step - 1, i, 0, part] = held[part, early]
                    forward[step - 1, i, 1, part] = held[part, late]

            late = jnp.maximum(picks_ref[s, 2 * count - 1 - me], 0)
            early = jnp.maximum(picks_ref[s, me], 0)
            for part in range(2):
                recv[0, part, s] = held[part, early]
                recv[1, part, s] = held[part, late]

            @pl.loop(1, GROUP)
            def _(i):
                d = plane * GROUP + lax.rem(column + i, GROUP)

                @pl.when(d > s + 1)
                def _():
                    passed(step, i, s, d).start()

                @pl.when(d <= s + 1)
                def _():
                    passed_single(step, i, s, d).start()

    ones_own = jnp.ones((2 * half, dim), BF16)
    row = lax.broadcasted_iota(jnp.int32, (half, 2 * half), 0)
    col = lax.broadcasted_iota(jnp.int32, (half, 2 * half), 1)
    for w in range(2):
        here = slice(w * subs, (w + 1) * subs)
        keys = jnp.concatenate([kv_ref[0, here], prev[w, 0]], axis=0).reshape(2 * half, dim)
        vals = jnp.concatenate([kv_ref[1, here], prev[w, 1]], axis=0).reshape(2 * half, dim)
        vals = jnp.concatenate([vals, ones_own], axis=1)
        usable = col <= row
        if w == 0:
            usable = usable | ((col >= half) & (me >= 1))
        else:
            usable = usable | (col >= half)
        for part in range(2):
            at = slice(part * span, (part + 1) * span)
            s = lax.dot_general(q_rot[w, at, :], keys, (((1,), (1,)), ((), ())),
                                preferred_element_type=F32)
            s = jnp.where(usable[None], s.reshape(-1, half, 2 * half), F32(-1e30)).reshape(span, -1)
            m = jnp.max(s, axis=-1, keepdims=True)
            p = jnp.exp2(((s - m) * scale).astype(BF16))
            acc[w, at, :] = jnp.dot(p, vals, preferred_element_type=F32)
            top[w, at, :] = jnp.broadcast_to(m, (span, dim))
        if w == 0:
            for step in range(DIRECT + 1, planes):
                relay(step)

    ones_far = jnp.ones((group * KB, dim), BF16)
    far_col = lax.broadcasted_iota(jnp.int32, (1, group * KB), 1)

    @pl.loop(0, count // group)
    def _(g):
        @pl.loop(g * group, (g + 1) * group)
        def _(s):
            mine = (s < (plane - DIRECT) * GROUP) & (lax.rem(s, GROUP) == column)

            @pl.when((s < me - 1) & jnp.logical_not(mine))
            def _():
                both(s, me).wait_recv()

            @pl.when((s >= me - 1) & (s != me) & jnp.logical_not(mine))
            def _():
                single(s, me).wait_recv()

        for w in range(2):
            limit = (me - 1) * KB if w == 0 else jnp.where(me == count - 1, (count - 1) * KB, count * KB)
            usable = far_col + g * (group * KB) < limit
            keys = recv[w, 0, pl.ds(g * group, group)].reshape(group * KB, dim)
            vals = recv[w, 1, pl.ds(g * group, group)].reshape(group * KB, dim)
            vals = jnp.concatenate([vals, ones_far], axis=1)
            for part in range(2):
                at = slice(part * span, (part + 1) * span)
                s = lax.dot_general(q_rot[w, at, :], keys, (((1,), (1,)), ((), ())),
                                    preferred_element_type=F32)
                s = jnp.where(usable, s, F32(-1e30))
                old = top[w, at, :]
                m = jnp.maximum(old, jnp.max(s, axis=-1, keepdims=True))
                p = jnp.exp2(((s - m[:, :1]) * scale).astype(BF16))
                keep = jnp.exp2((old - m) * scale)
                keep = jnp.concatenate([keep, keep], axis=1)
                acc[w, at, :] = acc[w, at, :] * keep + jnp.dot(p, vals, preferred_element_type=F32)
                top[w, at, :] = m

    for w in range(2):
        for h in range(heads):
            at = slice(h * half, (h + 1) * half)
            out_ref[w * half:(w + 1) * half, h * dim:(h + 1) * dim] = (
                acc[w, at, :dim] / acc[w, at, dim:]).astype(BF16)

    @pl.when(has_next)
    def _():
        neighbour(0, me + 1).wait_send()

    @pl.when(has_before)
    def _():
        neighbour(1, me - 1).wait_send()

    for step in range(DIRECT + 1, planes):
        @pl.when(plane + step < planes)
        def _():
            whole(step, me + step * GROUP).wait_send()

        @pl.when(plane >= step)
        def _():
            s = me - step * GROUP

            @pl.loop(1, GROUP)
            def _(i):
                d = plane * GROUP + lax.rem(column + i, GROUP)

                @pl.when(d > s + 1)
                def _():
                    passed(step, i, s, d).wait_send()

                @pl.when(d <= s + 1)
                def _():
                    passed_single(step, i, s, d).wait_send()

    @pl.loop(1, count)
    def _(i):
        d = peer(i)

        @pl.when(d > me + 1)
        def _():
            @pl.when(d // GROUP <= plane + DIRECT)
            def _():
                both(me, d).wait_send()

        @pl.when(d <= me + 1)
        def _():
            @pl.when(d // GROUP <= plane + DIRECT)
            def _():
                single(me, d).wait_send()


def per_device(queries, keys, values, basis, picks):
    half = queries.shape[0] // 2
    dim = basis.shape[0]
    heads = queries.shape[1] // dim
    count = lax.axis_size("pb")
    rows = heads * half
    planes = count // GROUP
    vmem = pl.BlockSpec(memory_space=pltpu.VMEM)
    made = pl.pallas_call(
        functools.partial(kernel, count, heads, dim, half),
        out_shape=pltpu.VMEM(queries.shape, BF16),
        in_specs=[pl.BlockSpec(memory_space=pl.ANY)] * 5,
        out_specs=vmem,
        scratch_shapes=[
            pltpu.VMEM(queries.shape, BF16),
            pltpu.VMEM((2, 2 * half // KB, KB, dim), BF16),
            pltpu.VMEM(basis.shape, BF16),
            pltpu.SMEM(picks.shape[::-1], jnp.int32),
            pltpu.VMEM((count, 2, 2, KB, dim), BF16),
            pltpu.VMEM((2, 2, count, KB, dim), BF16),
            pltpu.VMEM((2, 2, half // KB, KB, dim), BF16),
            pltpu.VMEM((2, rows, dim), BF16),
            pltpu.VMEM((2, rows, dim), F32),
            pltpu.VMEM((2, rows, 2 * dim), F32),
            pltpu.SemaphoreType.DMA((count,)),
            pltpu.SemaphoreType.DMA((count,)),
            pltpu.SemaphoreType.DMA((2,)),
            pltpu.SemaphoreType.DMA((2,)),
            pltpu.SemaphoreType.DMA((5,)),
            pltpu.VMEM((planes - 1, GROUP, 2, 2, KB, dim), BF16),
            pltpu.SemaphoreType.DMA((planes - 1, GROUP)),
            pltpu.SemaphoreType.DMA((planes - 1,)),
            pltpu.SemaphoreType.DMA((planes - 1,)),
            *[pltpu.VMEM((2, half // KB, KB, dim), BF16) for _ in range(planes - 1)],
        ],
        compiler_params=pltpu.CompilerParams(collective_id=0, has_side_effects=True),
        name="exchange_attend",
    )(queries, keys.reshape(-1, KB, dim), values.reshape(-1, KB, dim), basis, picks.T)
    return pl.pallas_call(
        place, out_shape=jax.ShapeDtypeStruct(queries.shape, BF16),
        in_specs=[vmem], out_specs=vmem, name="place_result")(pltpu.with_memory_space_constraint(made, pltpu.VMEM))


def place(a_ref, o_ref):
    o_ref[...] = a_ref[...]


def solution(mesh):
    in_specs = (P("pb", "grp"), P("pb", "grp"), P("pb", "grp"), P("grp", None), P("grp", None))
    out_specs = P("pb", "grp")
    return jax.shard_map(
        per_device, mesh=mesh, in_specs=in_specs, out_specs=out_specs, check_vma=False
    )
```

```python
import functools
import math

import jax
import jax.numpy as jnp
from jax import lax
from jax.experimental import pallas as pl
from jax.experimental.pallas import tpu as pltpu
from jax.sharding import PartitionSpec as P

KB = 32
GROUP = 4
DIRECT = 1
MESH = pl.DeviceIdType.MESH
F32 = jnp.float32
BF16 = jnp.bfloat16


def kernel(
    count, heads, dim, half,
    q_hbm, k_hbm, v_hbm, basis_hbm, picks_hbm, out_ref,
    q_ref, kv_ref, basis_ref, picks_ref,
    send, recv, prev, q_rot, top, acc, send_sem, recv_sem, prev_send, prev_recv, load_sem,
    forward, forward_send, raw_send, raw_recv, *raw,
):
    me = lax.axis_index("pb")
    group = min(16, count)
    span = heads // 2 * half
    planes = count // GROUP
    subs = half // KB
    plane, column = me // GROUP, lax.rem(me, GROUP)
    scale = dim ** (-0.5) * math.log2(math.e)

    def peer(i):
        return lax.rem(me + i, count)

    barrier = pltpu.get_barrier_semaphore()

    @pl.loop(1, count)
    def _(i):
        pl.semaphore_signal(barrier, inc=1, device_id={"pb": peer(i)}, device_id_type=MESH)


    pairs = ((picks_hbm, picks_ref), (k_hbm, kv_ref.at[0]), (v_hbm, kv_ref.at[1]),
             (q_hbm, q_ref), (basis_hbm, basis_ref))
    loads = [pltpu.make_async_copy(a, b, load_sem.at[i]) for i, (a, b) in enumerate(pairs)]
    for load in loads:
        load.start()
    for load in loads[:3]:
        load.wait()

    pl.semaphore_wait(barrier, count - 1)

    def whole(step, d):
        return pltpu.make_async_remote_copy(
            src_ref=kv_ref.at[:, pl.ds(0, subs)], dst_ref=raw[step - 1],
            send_sem=raw_send.at[step - 1], recv_sem=raw_recv.at[step - 1],
            device_id={"pb": d}, device_id_type=MESH)

    def passed(step, i, s, d):
        return pltpu.make_async_remote_copy(
            src_ref=forward.at[step - 1, i], dst_ref=recv.at[:, :, s],
            send_sem=forward_send.at[step - 1, i], recv_sem=recv_sem.at[s],
            device_id={"pb": d}, device_id_type=MESH)

    def passed_single(step, i, s, d):
        return pltpu.make_async_remote_copy(
            src_ref=forward.at[step - 1, i, 1], dst_ref=recv.at[1, :, s],
            send_sem=forward_send.at[step - 1, i], recv_sem=recv_sem.at[s],
            device_id={"pb": d}, device_id_type=MESH)

    def both(s, d):
        return pltpu.make_async_remote_copy(
            src_ref=send.at[d], dst_ref=recv.at[:, :, s], send_sem=send_sem.at[d],
            recv_sem=recv_sem.at[s], device_id={"pb": d}, device_id_type=MESH)

    def single(s, d):
        return pltpu.make_async_remote_copy(
            src_ref=send.at[d, 1], dst_ref=recv.at[1, :, s], send_sem=send_sem.at[d],
            recv_sem=recv_sem.at[s], device_id={"pb": d}, device_id_type=MESH)

    def neighbour(which, d):
        return pltpu.make_async_remote_copy(
            src_ref=kv_ref.at[:, pl.ds(which * subs, subs)], dst_ref=prev.at[which],
            send_sem=prev_send.at[which], recv_sem=prev_recv.at[which],
            device_id={"pb": d}, device_id_type=MESH)

    has_next = me < count - 1
    has_before = me > 0

    for step in range(planes - 1, DIRECT, -1):
        @pl.when(plane + step < planes)
        def _():
            whole(step, me + step * GROUP).start()

    @pl.when(has_next)
    def _():
        neighbour(0, me + 1).start()

    @pl.when(has_before)
    def _():
        neighbour(1, me - 1).start()

    @pl.loop(1, count)
    def _(i):
        d = peer(i)

        @pl.when(d // GROUP <= plane + DIRECT)
        def _():
            late = jnp.maximum(picks_ref[me, 2 * count - 1 - d], 0)
            send[d, 1, 0] = kv_ref[0, late]
            send[d, 1, 1] = kv_ref[1, late]

            @pl.when(d > me + 1)
            def _():
                early = jnp.maximum(picks_ref[me, d], 0)
                send[d, 0, 0] = kv_ref[0, early]
                send[d, 0, 1] = kv_ref[1, early]

    own = jnp.maximum(picks_ref[me, 2 * count - 1 - me], 0)
    recv[1, 0, me] = kv_ref[0, own]
    recv[1, 1, me] = kv_ref[1, own]

    @pl.loop(0, count)
    def _(s):
        @pl.when(s >= me - 1)
        def _():
            recv[0, 0, s] = jnp.zeros((KB, dim), BF16)
            recv[0, 1, s] = jnp.zeros((KB, dim), BF16)

    @pl.when(me == 0)
    def _():
        prev[0] = jnp.zeros((2, subs, KB, dim), BF16)

    @pl.when(me == count - 1)
    def _():
        prev[1] = kv_ref[:, :subs]

    @pl.loop(1, count)
    def _(i):
        d = peer(i)

        @pl.when(d > me + 1)
        def _():
            @pl.when(d // GROUP <= plane + DIRECT)
            def _():
                both(me, d).start()

        @pl.when(d <= me + 1)
        def _():
            @pl.when(d // GROUP <= plane + DIRECT)
            def _():
                single(me, d).start()

    loads[3].wait()
    loads[4].wait()
    basis = basis_ref[...]
    for w in range(2):
        for h in range(heads):
            q = q_ref[w * half:(w + 1) * half, h * dim:(h + 1) * dim]
            q_rot[w, h * half:(h + 1) * half, :] = jnp.dot(
                q, basis, preferred_element_type=F32).astype(BF16)

    @pl.when(has_before)
    def _():
        neighbour(0, me - 1).wait_recv()

    @pl.when(has_next)
    def _():
        neighbour(1, me + 1).wait_recv()

    def relay(step):
        s = me - step * GROUP
        held = raw[step - 1]

        @pl.when(plane >= step)
        def _():
            whole(step, s).wait_recv()

            @pl.loop(1, GROUP)
            def _(i):
                d = plane * GROUP + lax.rem(column + i, GROUP)
                late = jnp.maximum(picks_ref[s, 2 * count - 1 - d], 0)
                early = jnp.maximum(picks_ref[s, d], 0)
                for part in range(2):
                    forward[step - 1, i, 0, part] = held[part, early]
                    forward[step - 1, i, 1, part] = held[part, late]

            late = jnp.maximum(picks_ref[s, 2 * count - 1 - me], 0)
            early = jnp.maximum(picks_ref[s, me], 0)
            for part in range(2):
                recv[0, part, s] = held[part, early]
                recv[1, part, s] = held[part, late]

            @pl.loop(1, GROUP)
            def _(i):
                d = plane * GROUP + lax.rem(column + i, GROUP)

                @pl.when(d > s + 1)
                def _():
                    passed(step, i, s, d).start()

                @pl.when(d <= s + 1)
                def _():
                    passed_single(step, i, s, d).start()

    ones_own = jnp.ones((2 * half, dim), BF16)
    row = lax.broadcasted_iota(jnp.int32, (half, 2 * half), 0)
    col = lax.broadcasted_iota(jnp.int32, (half, 2 * half), 1)
    for w in range(2):
        here = slice(w * subs, (w + 1) * subs)
        keys = jnp.concatenate([kv_ref[0, here], prev[w, 0]], axis=0).reshape(2 * half, dim)
        vals = jnp.concatenate([kv_ref[1, here], prev[w, 1]], axis=0).reshape(2 * half, dim)
        vals = jnp.concatenate([vals, ones_own], axis=1)
        usable = col <= row
        if w == 0:
            usable = usable | ((col >= half) & (me >= 1))
        else:
            usable = usable | (col >= half)
        for part in range(2):
            at = slice(part * span, (part + 1) * span)
            s = lax.dot_general(q_rot[w, at, :], keys, (((1,), (1,)), ((), ())),
                                preferred_element_type=F32)
            s = jnp.where(usable[None], s.reshape(-1, half, 2 * half), F32(-1e30)).reshape(span, -1)
            m = jnp.max(s, axis=-1, keepdims=True)
            p = jnp.exp2(((s - m) * scale).astype(BF16))
            acc[w, at, :] = jnp.dot(p, vals, preferred_element_type=F32)
            top[w, at, :] = jnp.broadcast_to(m, (span, dim))
        if w == 0:
            for step in range(DIRECT + 1, planes):
                relay(step)

    ones_far = jnp.ones((group * KB, dim), BF16)
    far_col = lax.broadcasted_iota(jnp.int32, (1, group * KB), 1)

    @pl.loop(0, count // group)
    def _(g):
        @pl.loop(g * group, (g + 1) * group)
        def _(s):
            mine = (s < (plane - DIRECT) * GROUP) & (lax.rem(s, GROUP) == column)

            @pl.when((s < me - 1) & jnp.logical_not(mine))
            def _():
                both(s, me).wait_recv()

            @pl.when((s >= me - 1) & (s != me) & jnp.logical_not(mine))
            def _():
                single(s, me).wait_recv()

        for w in range(2):
            limit = (me - 1) * KB if w == 0 else jnp.where(me == count - 1, (count - 1) * KB, count * KB)
            usable = far_col + g * (group * KB) < limit
            keys = recv[w, 0, pl.ds(g * group, group)].reshape(group * KB, dim)
            vals = recv[w, 1, pl.ds(g * group, group)].reshape(group * KB, dim)
            vals = jnp.concatenate([vals, ones_far], axis=1)
            for part in range(2):
                at = slice(part * span, (part + 1) * span)
                s = lax.dot_general(q_rot[w, at, :], keys, (((1,), (1,)), ((), ())),
                                    preferred_element_type=F32)
                s = jnp.where(usable, s, F32(-1e30))
                old = top[w, at, :]
                m = jnp.maximum(old, jnp.max(s, axis=-1, keepdims=True))
                p = jnp.exp2(((s - m[:, :1]) * scale).astype(BF16))
                keep = jnp.exp2((old - m) * scale)
                keep = jnp.concatenate([keep, keep], axis=1)
                summed = acc[w, at, :] * keep + jnp.dot(p, vals, preferred_element_type=F32)
                if count == group:
                    result = (summed[:, :dim] / summed[:, dim:]).astype(BF16)
                    for i in range(heads // 2):
                        h = part * (heads // 2) + i
                        out_ref[w * half:(w + 1) * half, h * dim:(h + 1) * dim] = (
                            result[i * half:(i + 1) * half])
                else:
                    acc[w, at, :] = summed
                    top[w, at, :] = m

    for w in range(2 if count > group else 0):
        for h in range(heads):
            at = slice(h * half, (h + 1) * half)
            out_ref[w * half:(w + 1) * half, h * dim:(h + 1) * dim] = (
                acc[w, at, :dim] / acc[w, at, dim:]).astype(BF16)

    @pl.when(has_next)
    def _():
        neighbour(0, me + 1).wait_send()

    @pl.when(has_before)
    def _():
        neighbour(1, me - 1).wait_send()

    for step in range(DIRECT + 1, planes):
        @pl.when(plane + step < planes)
        def _():
            whole(step, me + step * GROUP).wait_send()

        @pl.when(plane >= step)
        def _():
            s = me - step * GROUP

            @pl.loop(1, GROUP)
            def _(i):
                d = plane * GROUP + lax.rem(column + i, GROUP)

                @pl.when(d > s + 1)
                def _():
                    passed(step, i, s, d).wait_send()

                @pl.when(d <= s + 1)
                def _():
                    passed_single(step, i, s, d).wait_send()

    @pl.loop(1, count)
    def _(i):
        d = peer(i)

        @pl.when(d > me + 1)
        def _():
            @pl.when(d // GROUP <= plane + DIRECT)
            def _():
                both(me, d).wait_send()

        @pl.when(d <= me + 1)
        def _():
            @pl.when(d // GROUP <= plane + DIRECT)
            def _():
                single(me, d).wait_send()


def per_device(queries, keys, values, basis, picks):
    half = queries.shape[0] // 2
    dim = basis.shape[0]
    heads = queries.shape[1] // dim
    count = lax.axis_size("pb")
    rows = heads * half
    planes = count // GROUP
    vmem = pl.BlockSpec(memory_space=pltpu.VMEM)
    made = pl.pallas_call(
        functools.partial(kernel, count, heads, dim, half),
        out_shape=pltpu.VMEM(queries.shape, BF16),
        in_specs=[pl.BlockSpec(memory_space=pl.ANY)] * 5,
        out_specs=vmem,
        scratch_shapes=[
            pltpu.VMEM(queries.shape, BF16),
            pltpu.VMEM((2, 2 * half // KB, KB, dim), BF16),
            pltpu.VMEM(basis.shape, BF16),
            pltpu.SMEM(picks.shape[::-1], jnp.int32),
            pltpu.VMEM((count, 2, 2, KB, dim), BF16),
            pltpu.VMEM((2, 2, count, KB, dim), BF16),
            pltpu.VMEM((2, 2, half // KB, KB, dim), BF16),
            pltpu.VMEM((2, rows, dim), BF16),
            pltpu.VMEM((2, rows, dim), F32),
            pltpu.VMEM((2, rows, 2 * dim), F32),
            pltpu.SemaphoreType.DMA((count,)),
            pltpu.SemaphoreType.DMA((count,)),
            pltpu.SemaphoreType.DMA((2,)),
            pltpu.SemaphoreType.DMA((2,)),
            pltpu.SemaphoreType.DMA((5,)),
            pltpu.VMEM((planes - 1, GROUP, 2, 2, KB, dim), BF16),
            pltpu.SemaphoreType.DMA((planes - 1, GROUP)),
            pltpu.SemaphoreType.DMA((planes - 1,)),
            pltpu.SemaphoreType.DMA((planes - 1,)),
            *[pltpu.VMEM((2, half // KB, KB, dim), BF16) for _ in range(planes - 1)],
        ],
        compiler_params=pltpu.CompilerParams(collective_id=0, has_side_effects=True),
        name="exchange_attend",
    )(queries, keys.reshape(-1, KB, dim), values.reshape(-1, KB, dim), basis, picks.T)
    return pl.pallas_call(
        place, out_shape=jax.ShapeDtypeStruct(queries.shape, BF16),
        in_specs=[vmem], out_specs=vmem, name="place_result")(pltpu.with_memory_space_constraint(made, pltpu.VMEM))


def place(a_ref, o_ref):
    o_ref[...] = a_ref[...]


def solution(mesh):
    in_specs = (P("pb", "grp"), P("pb", "grp"), P("pb", "grp"), P("grp", None), P("grp", None))
    out_specs = P("pb", "grp")
    return jax.shard_map(
        per_device, mesh=mesh, in_specs=in_specs, out_specs=out_specs, check_vma=False
    )
```
